128 devices in a mesh: group: 4 (over y), dom: 32 (over x, z, core).
Axes of the slice: x: 4, y: 4, z: 4, core: 2. Of those that a mesh axis runs over, the one named last changes fastest.
Arguments:
- mode_shapes: float32 [96, 262144], P(None, ('group', 'dom')), may hold values from -6 to 6
- send_nodes: int32 [128, 4096], P(('group', 'dom')), may hold values from 0 to 2047, as said below
- interp_index: int32 [8, 64, 16384], P(None, 'group', 'dom'), may hold values from -1 to 4095, as said below
- interp_weight: float32 [8, 64, 16384], P(None, 'group', 'dom'), may hold values from 0.1 to 1
- blend: float32 [64, 16384], P('group', 'dom'), may hold values from 0.2 to 1
- motion_gain: float32 [30, 64, 16384], P(None, 'group', 'dom'), may hold values from -3 to 3
- frequency: float32 [32], replicated, may hold values from 0.3 to 3
- volume: float32 [64, 16384], P('group', 'dom'), may hold values from 0.5 to 2
- jacobian: float32 [125, 64, 16384], P(None, 'group', 'dom'), may hold values from -1.2 to 1.2
- state: bfloat16 [320, 64, 16384], P(None, 'group', 'dom'), may hold values from -6 to 6
Outputs:
- mesh_motion: float32 [96, 64, 16384], P(None, 'group', 'dom')
- residual: float32 [320, 64, 16384], P(None, 'group', 'dom')
The draws below stay inside these ranges and needn't reach their ends.
Inputs may be any that keep to these rules, and one draw needn't show every extreme that they name: `send_nodes`: each entry names a node local to the owner of its row, 0 to 2047. `interp_index`: A live entry is s * 32 + t, naming slot t that owner s sends to the cell's partition; a cell has 1 to 8 live entries, stored first, then -1 for padding; some cell has all 8 live. From each owner a partition uses at most 32 slots.
All inputs are finite; a program needn't handle non-finite values.
Results may differ from the reference program's by a relative error of at most 0.0003.
Values may be sent and summed in bfloat16 or wider, within the bound.
A program may use at most 192 MiB of HBM per device.

```python
import math
import jax
import jax.numpy as jnp

COMP = 3
VARS = 5
KST = 8
SLOT = 32
NS_DEV = 2048
BI = 16
BJ = 512
CASES = 32
NS = 262144
NI = 64
NJ = 16384
N_DOM = 32
DEVICES = 128


def coupling_tables(key):
    keys = jax.random.split(jax.random.fold_in(key, 7), 9)
    load = jax.random.randint(keys[0], (DEVICES,), 2, 6)
    base = jax.random.randint(keys[1], (DEVICES, DEVICES), 0, SLOT // 2 + 1)
    counts = jnp.clip(base * load[None, :] // 2, 1, SLOT)
    first_src = jax.random.randint(keys[2], (), 0, DEVICES)
    first_dst = jax.random.randint(keys[3], (), 0, DEVICES)
    full_dst = jax.random.randint(keys[4], (), 0, DEVICES)
    source = jnp.arange(DEVICES)[:, None]
    target = jnp.arange(DEVICES)[None, :]
    counts = jnp.where((source == first_src) & (target == first_dst) | (target == full_dst), SLOT, counts)
    counts = jnp.where((source == DEVICES - 1) & (target == 0), SLOT, counts)
    nodes = jax.random.randint(keys[5], (DEVICES, DEVICES * SLOT), 0, NS_DEV).astype(jnp.int32)
    nlive = jax.random.randint(keys[6], (NI, NJ), 1, KST + 1)
    nlive = nlive.at[0, 0].set(KST)
    owners = jax.random.randint(keys[7], (KST, NI, NJ), 0, DEVICES)
    cell_part = (jnp.arange(NI) // BI)[:, None] * N_DOM + (jnp.arange(NJ) // BJ)[None, :]
    avail = counts[owners, jnp.broadcast_to(cell_part[None], (KST, NI, NJ))]
    pick = jax.random.randint(keys[8], (KST, NI, NJ), 0, 1 << 20) % avail
    flat = owners * SLOT + pick
    order = jnp.arange(KST)[:, None, None]
    index = jnp.where(order < nlive[None], flat, -1).astype(jnp.int32)
    full_index = index.at[0, 0, 0].set(DEVICES * SLOT - 1)
    return (nodes, full_index)


def draw_send_nodes(key, part):
    return coupling_tables(key)[0]


def draw_interp_index(key, part):
    return coupling_tables(key)[1]


def steps_of(stream_key, extent, shards, smallest, top_value):
    def one(position, shards_of):
        draws = jax.random.uniform(jax.random.fold_in(jax.random.fold_in(stream_key, 6), position), (shards_of,), jnp.float32, smallest / len(shards), top_value / len(shards))
        return jnp.repeat(jnp.exp(draws), extent[position] // shards_of).reshape((-1,) + (1,) * (len(extent) - position - 1))

    loudness = one(*shards[0])
    for cut in shards[1:]:
        loudness = loudness * one(*cut)
    return loudness


def bell_draw(rng, shape, width, most, cuts=(), kind=jnp.bfloat16):
    entries = width * jax.random.normal(rng, shape, jnp.float32)
    if cuts:
        entries = entries * steps_of(rng, shape, cuts, -0.22, 0.18)
    return jnp.clip(entries, -most, most).astype(kind)


def setup_inputs(seed: int = 0) -> dict:
    arg_keys = jax.random.split(jax.random.key(seed), 11)
    return {
        "mode_shapes": bell_draw(arg_keys[0], (CASES * COMP, NS), 1.0, 6.0, ((1, 128),), jnp.float32),
        "send_nodes": draw_send_nodes(jax.random.fold_in(arg_keys[10], 71), 0),
        "interp_index": draw_interp_index(jax.random.fold_in(arg_keys[10], 71), 0),
        "interp_weight": jnp.clip(0.1 + 0.9 * jax.random.uniform(arg_keys[3], (KST, NI, NJ), jnp.float32) ** steps_of(arg_keys[3], (KST, NI, NJ), ((1, 4), (2, 32)), -0.2, 0.2), 0.1, 1.0),
        "blend": jnp.clip(0.2 + 0.8 * jax.random.uniform(arg_keys[4], (NI, NJ), jnp.float32) ** steps_of(arg_keys[4], (NI, NJ), ((0, 4), (1, 32)), -0.2, 0.2), 0.2, 1.0),
        "motion_gain": bell_draw(arg_keys[5], (2 * VARS * COMP, NI, NJ), 0.5, 3.0, ((1, 4), (2, 32)), jnp.float32),
        "frequency": jnp.clip(jnp.exp(jax.random.uniform(arg_keys[6], (CASES,), jnp.float32, math.log(0.3), math.log(3.0))), 0.3, 3.0),
        "volume": jnp.clip(jnp.exp(math.log(2.0) - 1.3862944 * jax.random.uniform(arg_keys[7], (NI, NJ), jnp.float32) ** steps_of(arg_keys[7], (NI, NJ), ((0, 4), (1, 32)), -0.2, 0.2)), 0.5, 2.0),
        "jacobian": bell_draw(arg_keys[8], (5 * VARS * VARS, NI, NJ), 0.2, 1.2, ((1, 4), (2, 32)), jnp.float32),
        "state": bell_draw(arg_keys[9], (CASES * 2 * VARS, NI, NJ), 1.0, 6.0, ((1, 4), (2, 32))),
    }


def apply_block(block, field):
    total = jnp.zeros(field.shape, jnp.float32)
    for u in range(VARS):
        total = total + block[:, u][None, None] * field[:, :, u][:, :, None]
    return total


def reference(mode_shapes, send_nodes, interp_index, interp_weight, blend, motion_gain, frequency, volume, jacobian, state):
    rows = jnp.arange(NI, dtype=jnp.int32) // BI
    cols = jnp.arange(NJ, dtype=jnp.int32) // BJ
    partition = rows[:, None] * N_DOM + cols[None, :]
    live = interp_index >= 0
    safe = jnp.maximum(interp_index, 0)
    weight = jnp.where(live, interp_weight, jnp.float32(0.0))
    scaled = weight * (blend / jnp.sum(weight, axis=0))[None]
    motion = jnp.zeros((CASES * COMP, NI, NJ), jnp.float32)
    for k in range(KST):
        owner = safe[k] // SLOT
        slot = safe[k] % SLOT
        node = send_nodes[owner, partition * SLOT + slot] + owner * NS_DEV
        motion = motion + scaled[k][None] * mode_shapes[:, node]
    gain = motion_gain.reshape(2, VARS, COMP, NI, NJ)
    disp = motion.reshape(CASES, COMP, NI, NJ)
    pos_force = jnp.zeros((CASES, VARS, NI, NJ), jnp.float32)
    vel_force = jnp.zeros((CASES, VARS, NI, NJ), jnp.float32)
    for x in range(COMP):
        pos_force = pos_force + gain[0, :, x][None] * disp[:, x][:, None]
        vel_force = vel_force + gain[1, :, x][None] * disp[:, x][:, None]
    field = state.astype(jnp.float32).reshape(CASES, 2, VARS, NI, NJ)
    blocks = jacobian.reshape(5, VARS, VARS, NI, NJ)
    padded = jnp.pad(field, ((0, 0), (0, 0), (0, 0), (1, 1), (1, 1)))
    flux = apply_block(blocks[0], field)
    flux = flux + apply_block(blocks[1], padded[:, :, :, :-2, 1:-1])
    flux = flux + apply_block(blocks[2], padded[:, :, :, 2:, 1:-1])
    flux = flux + apply_block(blocks[3], padded[:, :, :, 1:-1, :-2])
    flux = flux + apply_block(blocks[4], padded[:, :, :, 1:-1, 2:])
    omega = frequency[:, None, None, None]
    real_part = flux[:, 0] - omega * volume[None, None] * field[:, 1] + pos_force
    imag_part = flux[:, 1] + omega * volume[None, None] * field[:, 0] + omega * vel_force
    residual = jnp.stack([real_part, imag_part], axis=1).reshape(CASES * 2 * VARS, NI, NJ)
    return motion, residual
```

```python
import functools

import jax
import jax.numpy as jnp
from jax import lax
from jax.experimental import pallas as pl
from jax.experimental.pallas import tpu as pltpu
from jax.sharding import PartitionSpec as P

COMP = 3
VARS = 5
CASES = 32
KST = 8
SLOT = 32
BI = 16
BJ = 512
LANES = 128
ROWS = CASES * 2 * VARS
TILES = BJ // LANES
HALO_ROWS = 32
CASE_ROWS = 2 * VARS
CG = 4
R2 = CG * CASE_ROWS
PITCH = 32
RPITCH = (TILES + 2) * PITCH


def halo_kernel(st_ref, first_ref, last_ref, left_ref, right_ref, scr):
    n = HALO_ROWS * BI
    for t in range(TILES):
        tile = st_ref[:, :, t * LANES:(t + 1) * LANES].astype(jnp.float32)
        scr[t] = tile.reshape(n, LANES)
    for t in range(TILES):
        lanes = slice(t * LANES, (t + 1) * LANES)
        top = scr.at[t][pl.ds(0, HALO_ROWS, stride=BI), :]
        bottom = scr.at[t][pl.ds(BI - 1, HALO_ROWS, stride=BI), :]
        first_ref[:, lanes] = top.astype(jnp.bfloat16)
        last_ref[:, lanes] = bottom.astype(jnp.bfloat16)
    lane = lax.broadcasted_iota(jnp.int32, (16, LANES), 1)
    dims = (((1,), (1,)), ((), ()))
    pick = jnp.where(lane == 0, 1.0, 0.0).astype(jnp.bfloat16)
    edge = st_ref[:, :, 0:LANES].reshape(n, LANES)
    left_ref[...] = lax.dot_general(pick, edge, dims, preferred_element_type=jnp.float32)[0:1]
    pick = jnp.where(lane == LANES - 1, 1.0, 0.0).astype(jnp.bfloat16)
    edge = st_ref[:, :, BJ - LANES:BJ].reshape(n, LANES)
    right_ref[...] = lax.dot_general(pick, edge, dims, preferred_element_type=jnp.float32)[0:1]


def halo_strips(state):
    steps = ROWS // HALO_ROWS
    return pl.pallas_call(
        halo_kernel,
        grid=(steps,),
        in_specs=[pl.BlockSpec((HALO_ROWS, BI, BJ), lambda i: (i, 0, 0))],
        out_specs=[
            pl.BlockSpec((HALO_ROWS, BJ), lambda i: (i, 0)),
            pl.BlockSpec((HALO_ROWS, BJ), lambda i: (i, 0)),
            pl.BlockSpec((1, HALO_ROWS * BI), lambda i: (0, i)),
            pl.BlockSpec((1, HALO_ROWS * BI), lambda i: (0, i)),
        ],
        out_shape=[
            jax.ShapeDtypeStruct((ROWS, BJ), jnp.bfloat16),
            jax.ShapeDtypeStruct((ROWS, BJ), jnp.bfloat16),
            jax.ShapeDtypeStruct((1, ROWS * BI), jnp.float32),
            jax.ShapeDtypeStruct((1, ROWS * BI), jnp.float32),
        ],
        scratch_shapes=[pltpu.VMEM((TILES, HALO_ROWS * BI, LANES), jnp.float32)],
        cost_estimate=pl.CostEstimate(flops=4_000_000, bytes_accessed=6_000_000, transcendentals=0),
        name="halo_strips",
    )(state)


def merge_rows(table_ref, entries, sub):
    total = None
    for m, entry in enumerate(entries):
        row = table_ref[pl.ds(entry, 8, stride=0), :]
        total = row if total is None else jnp.where(sub == m, row, total)
    return total


def pick_kernel(nodes_ref, ms_ref, out_ref, tab, *, count):
    nodes = ms_ref.shape[1]
    for b in range(nodes // LANES):
        block = ms_ref[:, b * LANES:(b + 1) * LANES]
        padded = jnp.concatenate([block, jnp.zeros((LANES - CASES * COMP, LANES), jnp.float32)], axis=0)
        tab[b * LANES:(b + 1) * LANES, :] = padded.T
    sub = lax.broadcasted_iota(jnp.int32, (8, LANES), 0)

    @pl.loop(0, count // 32)
    def _(b):
        for g in range(4):
            entries = [nodes_ref[b * 32 + g * 8 + m] for m in range(8)]
            out_ref[b, g * 8:(g + 1) * 8, :] = merge_rows(tab, entries, sub)


def picked_rows(mode_shapes, send_nodes):
    count = send_nodes.shape[1]
    nodes = mode_shapes.shape[1]
    return pl.pallas_call(
        functools.partial(pick_kernel, count=count),
        in_specs=[pl.BlockSpec(memory_space=pltpu.SMEM), pl.BlockSpec(memory_space=pltpu.VMEM)],
        out_specs=pl.BlockSpec(memory_space=pltpu.VMEM),
        out_shape=jax.ShapeDtypeStruct((count // SLOT, SLOT, LANES), jnp.float32),
        scratch_shapes=[pltpu.VMEM((nodes, LANES), jnp.float32)],
        cost_estimate=pl.CostEstimate(flops=1_000_000, bytes_accessed=3_000_000, transcendentals=0),
        name="picked_rows",
    )(send_nodes.reshape(count), mode_shapes)


def flux_kernel(freq_ref, st_ref, up_ref, dn_ref, lf_ref, rt_ref, vol_ref, jac_ref, out_ref, q):
    step = pl.program_id(0)
    lane8 = lax.broadcasted_iota(jnp.int32, (8, LANES), 1)
    row8 = lax.broadcasted_iota(jnp.int32, (8, LANES), 0)
    dims = (((0,), (0,)), ((), ()))

    def outer(ref, at):
        values = jnp.broadcast_to(ref[...], (8, R2 * BI))
        spot = jnp.where((row8 == 0) & (lane8 == at), 1.0, 0.0)
        return lax.dot_general(values.astype(jnp.bfloat16), spot.astype(jnp.bfloat16), dims, preferred_element_type=jnp.float32)

    left = outer(lf_ref, LANES - 1)
    right = outer(rt_ref, 0)
    for r in range(R2):
        q[r * RPITCH + 8:r * RPITCH + 8 + BI, :] = left[r * BI:(r + 1) * BI]
        base = r * RPITCH + (TILES + 1) * PITCH + 8
        q[base:base + BI, :] = right[r * BI:(r + 1) * BI]
        for t in range(TILES):
            base = r * RPITCH + (t + 1) * PITCH + 8
            q[base:base + BI, :] = st_ref[r, :, t * LANES:(t + 1) * LANES].astype(jnp.float32)
    for t in range(TILES):
        lanes = slice(t * LANES, (t + 1) * LANES)
        base = (t + 1) * PITCH
        q[pl.ds(base + 7, R2, stride=RPITCH), :] = up_ref[:, lanes].astype(jnp.float32)
        q[pl.ds(base + 8 + BI, R2, stride=RPITCH), :] = dn_ref[:, lanes].astype(jnp.float32)

    first_lane = lane8 == 0
    last_lane = lane8 == LANES - 1

    @pl.loop(0, 2 * TILES * (CG // 2))
    def _(it):
        pair = it // (2 * TILES)
        pos = it % (2 * TILES)
        ti = pos // TILES
        tj = pos % TILES
        irows = pl.ds(pl.multiple_of(ti * 8, 8), 8)
        jlanes = pl.ds(pl.multiple_of(tj * LANES, LANES), LANES)
        base = pair * (2 * CASE_ROWS * RPITCH) + (tj + 1) * PITCH + 8 + ti * 8
        sets = [(cs, part) for cs in range(2) for part in range(2)]
        acc = [[None] * VARS for _ in sets]
        centers = {}

        def load(index, u, shift):
            r = index * VARS + u
            return q[pl.ds(base + r * RPITCH + shift, 8), :]

        for u in range(VARS):
            for b in range(5):
                values = []
                for index in range(4):
                    if b == 0:
                        x = load(index, u, 0)
                    elif b == 1:
                        x = load(index, u, -1)
                    elif b == 2:
                        x = load(index, u, 1)
                    elif b == 3:
                        here = pltpu.roll(load(index, u, 0), 1, 1)
                        x = jnp.where(first_lane, pltpu.roll(load(index, u, -PITCH), 1, 1), here)
                    else:
                        here = pltpu.roll(load(index, u, 0), LANES - 1, 1)
                        x = jnp.where(last_lane, pltpu.roll(load(index, u, PITCH), LANES - 1, 1), here)
                    values.append(x)
                for v in range(VARS):
                    block = jac_ref[b * VARS * VARS + v * VARS + u, irows, jlanes]
                    for index in range(4):
                        term = block * values[index]
                        old = acc[index][v]
                        acc[index][v] = term if old is None else old + term
        volume = vol_ref[irows, jlanes]
        for cs in range(2):
            scale = volume * freq_ref[step * CG + pair * 2 + cs]
            for v in range(VARS):
                real = load(cs * 2, v, 0)
                imag = load(cs * 2 + 1, v, 0)
                row = (pair * 2 + cs) * CASE_ROWS + v
                out_ref[row, irows, jlanes] = acc[cs * 2][v] - scale * imag
                out_ref[row + VARS, irows, jlanes] = acc[cs * 2 + 1][v] + scale * real


def flux_part(frequency, state, up, down, left, right, volume, jacobian):
    steps = CASES // CG
    whole = lambda i: (0, 0)
    return pl.pallas_call(
        flux_kernel,
        grid=(steps,),
        in_specs=[
            pl.BlockSpec(memory_space=pltpu.SMEM),
            pl.BlockSpec((R2, BI, BJ), lambda i: (i, 0, 0)),
            pl.BlockSpec((R2, BJ), lambda i: (i, 0)),
            pl.BlockSpec((R2, BJ), lambda i: (i, 0)),
            pl.BlockSpec((1, R2 * BI), lambda i: (0, i)),
            pl.BlockSpec((1, R2 * BI), lambda i: (0, i)),
            pl.BlockSpec((BI, BJ), whole),
            pl.BlockSpec((5 * VARS * VARS, BI, BJ), lambda i: (0, 0, 0)),
        ],
        out_specs=pl.BlockSpec((R2, BI, BJ), lambda i: (i, 0, 0)),
        out_shape=jax.ShapeDtypeStruct((ROWS, BI, BJ), jnp.float32),
        scratch_shapes=[pltpu.VMEM((R2 * RPITCH, LANES), jnp.float32)],
        cost_estimate=pl.CostEstimate(flops=140_000_000, bytes_accessed=20_000_000, transcendentals=0),
        name="flux_part",
    )(frequency, state, up, down, left, right, volume, jacobian)


def spread_kernel(freq_ref, entry_ref, index_ref, weight_ref, blend_ref, gain_ref, table_ref, flux_ref, motion_ref, out_ref, wsc, wt, acc, disp):
    total = jnp.zeros((8, LANES), jnp.float32)
    for k in range(KST):
        total = total + jnp.where(index_ref[k] >= 0, weight_ref[k], 0.0)
    ratio = blend_ref[...] / total
    for k in range(KST):
        wsc[k * 8:(k + 1) * 8, :] = jnp.where(index_ref[k] >= 0, weight_ref[k], 0.0) * ratio
    sub = lax.broadcasted_iota(jnp.int32, (8, LANES), 0)

    @pl.loop(0, 8)
    def _(s):
        mine = wsc[pl.ds(s, KST, stride=8), :]
        wide = jnp.concatenate([mine, jnp.zeros((LANES - KST, LANES), jnp.float32)], axis=0)
        wt[...] = wide.T

        @pl.loop(0, LANES // 8)
        def _(jb):
            rows = pl.ds(pl.multiple_of(jb * 8, 8), 8)
            wide8 = wt[rows, :]
            sums = None
            for k in range(KST):
                entries = [entry_ref[0, k * 8 + s, jb * 8 + m] for m in range(8)]
                value = merge_rows(table_ref, entries, sub) * jnp.broadcast_to(wide8[:, k:k + 1], (8, LANES))
                sums = value if sums is None else sums + value
            acc[rows, :] = sums

        turned = acc[...].T
        for g in range(CASES * COMP // 8):
            disp[pl.ds(g * 64 + s, 8, stride=8), :] = turned[g * 8:(g + 1) * 8]

    gains = [gain_ref[i] for i in range(2 * VARS * COMP)]

    @pl.loop(0, CASES)
    def _(c):
        freq = freq_ref[c]
        parts = [disp[pl.ds(pl.multiple_of((c * COMP + x) * 8, 8), 8), :] for x in range(COMP)]
        for x in range(COMP):
            motion_ref[c * COMP + x] = parts[x]
        for v in range(VARS):
            pos = gains[v * COMP] * parts[0]
            vel = gains[(VARS + v) * COMP] * parts[0]
            for x in range(1, COMP):
                pos = pos + gains[v * COMP + x] * parts[x]
                vel = vel + gains[(VARS + v) * COMP + x] * parts[x]
            row = c * CASE_ROWS + v
            out_ref[row] = flux_ref[row] + pos
            out_ref[row + VARS] = flux_ref[row + VARS] + freq * vel


def spread_cells(frequency, entries, index, weight, blend, gain, table, flux):
    place = lambda i: (0, i // TILES, i % TILES)
    flat = lambda i: (i // TILES, i % TILES)
    return pl.pallas_call(
        spread_kernel,
        grid=(2 * TILES,),
        in_specs=[
            pl.BlockSpec(memory_space=pltpu.SMEM),
            pl.BlockSpec((1, KST * 8, LANES), lambda i: (i, 0, 0), memory_space=pltpu.SMEM),
            pl.BlockSpec((KST, 8, LANES), place),
            pl.BlockSpec((KST, 8, LANES), place),
            pl.BlockSpec((8, LANES), flat),
            pl.BlockSpec((2 * VARS * COMP, 8, LANES), place),
            pl.BlockSpec(table.shape, lambda i: (0, 0)),
            pl.BlockSpec((ROWS, 8, LANES), place),
        ],
        out_specs=[
            pl.BlockSpec((CASES * COMP, 8, LANES), place),
            pl.BlockSpec((ROWS, 8, LANES), place),
        ],
        out_shape=[
            jax.ShapeDtypeStruct((CASES * COMP, BI, BJ), jnp.float32),
            jax.ShapeDtypeStruct((ROWS, BI, BJ), jnp.float32),
        ],
        scratch_shapes=[
            pltpu.VMEM((KST * 8, LANES), jnp.float32),
            pltpu.VMEM((LANES, LANES), jnp.float32),
            pltpu.VMEM((LANES, LANES), jnp.float32),
            pltpu.VMEM((CASES * COMP * 8, LANES), jnp.float32),
        ],
        cost_estimate=pl.CostEstimate(flops=40_000_000, bytes_accessed=28_000_000, transcendentals=0),
        name="spread_cells",
    )(frequency, entries, index, weight, blend, gain, table, flux)


def shifted(value, axis, up):
    peers = lax.axis_size(axis)
    pairs = [(i, i + 1) for i in range(peers - 1)]
    return lax.ppermute(value, axis, pairs if up else [(j, i) for i, j in pairs])


def local(mode_shapes, send_nodes, interp_index, interp_weight, blend, motion_gain, frequency, volume, jacobian, state):
    first, last, left_col, right_col = halo_strips(state)
    up = shifted(last, "group", True)
    down = shifted(first, "group", False)
    left = shifted(right_col, "dom", True)
    right = shifted(left_col, "dom", False)
    outgoing = picked_rows(mode_shapes, send_nodes)
    arrived = lax.all_to_all(outgoing, ("group", "dom"), split_axis=0, concat_axis=0, tiled=True)
    table = arrived.reshape(-1, LANES)
    safe = jnp.maximum(interp_index, 0)
    entries = safe.reshape(KST, 2, 8, TILES, LANES).transpose(1, 3, 0, 2, 4).reshape(2 * TILES, KST * 8, LANES)
    flux = flux_part(frequency, state, up, down, left, right, volume, jacobian)
    return tuple(spread_cells(frequency, entries, interp_index, interp_weight, blend, motion_gain, table, flux))


def solution(mesh):
    placed = (
        P(None, ("group", "dom")),
        P(("group", "dom"), None),
        P(None, "group", "dom"),
        P(None, "group", "dom"),
        P("group", "dom"),
        P(None, "group", "dom"),
        P(),
        P("group", "dom"),
        P(None, "group", "dom"),
        P(None, "group", "dom"),
    )
    return jax.shard_map(
        local,
        mesh=mesh,
        in_specs=placed,
        out_specs=(P(None, "group", "dom"), P(None, "group", "dom")),
        check_vma=False,
    )
```

```python
import functools

import jax
import jax.numpy as jnp
from jax import lax
from jax.experimental import pallas as pl
from jax.experimental.pallas import tpu as pltpu
from jax.sharding import PartitionSpec as P

COMP = 3
VARS = 5
CASES = 32
KST = 8
SLOT = 32
BI = 16
BJ = 512
LANES = 128
ROWS = CASES * 2 * VARS
TILES = BJ // LANES
HALO_ROWS = 32
CASE_ROWS = 2 * VARS
CG = 4
R2 = CG * CASE_ROWS
PITCH = 32
RPITCH = (TILES + 2) * PITCH


def halo_kernel(st_ref, first_ref, last_ref, left_ref, right_ref, scr):
    n = HALO_ROWS * BI
    for t in range(TILES):
        tile = st_ref[:, :, t * LANES:(t + 1) * LANES].astype(jnp.float32)
        scr[t] = tile.reshape(n, LANES)
    for t in range(TILES):
        lanes = slice(t * LANES, (t + 1) * LANES)
        top = scr.at[t][pl.ds(0, HALO_ROWS, stride=BI), :]
        bottom = scr.at[t][pl.ds(BI - 1, HALO_ROWS, stride=BI), :]
        first_ref[:, lanes] = top.astype(jnp.bfloat16)
        last_ref[:, lanes] = bottom.astype(jnp.bfloat16)
    lane = lax.broadcasted_iota(jnp.int32, (16, LANES), 1)
    dims = (((1,), (1,)), ((), ()))
    pick = jnp.where(lane == 0, 1.0, 0.0).astype(jnp.bfloat16)
    edge = st_ref[:, :, 0:LANES].reshape(n, LANES)
    left_ref[...] = lax.dot_general(pick, edge, dims, preferred_element_type=jnp.float32)[0:1]
    pick = jnp.where(lane == LANES - 1, 1.0, 0.0).astype(jnp.bfloat16)
    edge = st_ref[:, :, BJ - LANES:BJ].reshape(n, LANES)
    right_ref[...] = lax.dot_general(pick, edge, dims, preferred_element_type=jnp.float32)[0:1]


def halo_strips(state):
    steps = ROWS // HALO_ROWS
    return pl.pallas_call(
        halo_kernel,
        grid=(steps,),
        in_specs=[pl.BlockSpec((HALO_ROWS, BI, BJ), lambda i: (i, 0, 0))],
        out_specs=[
            pl.BlockSpec((HALO_ROWS, BJ), lambda i: (i, 0)),
            pl.BlockSpec((HALO_ROWS, BJ), lambda i: (i, 0)),
            pl.BlockSpec((1, HALO_ROWS * BI), lambda i: (0, i)),
            pl.BlockSpec((1, HALO_ROWS * BI), lambda i: (0, i)),
        ],
        out_shape=[
            jax.ShapeDtypeStruct((ROWS, BJ), jnp.bfloat16),
            jax.ShapeDtypeStruct((ROWS, BJ), jnp.bfloat16),
            jax.ShapeDtypeStruct((1, ROWS * BI), jnp.float32),
            jax.ShapeDtypeStruct((1, ROWS * BI), jnp.float32),
        ],
        scratch_shapes=[pltpu.VMEM((TILES, HALO_ROWS * BI, LANES), jnp.float32)],
        cost_estimate=pl.CostEstimate(flops=4_000_000, bytes_accessed=6_000_000, transcendentals=0),
        name="halo_strips",
    )(state)


def merge_rows(table_ref, entries, sub):
    total = None
    for m, entry in enumerate(entries):
        row = table_ref[pl.ds(entry, 8, stride=0), :]
        total = row if total is None else jnp.where(sub == m, row, total)
    return total


def pick_kernel(nodes_ref, ms_ref, out_ref, tab, *, count):
    nodes = ms_ref.shape[1]
    for b in range(nodes // LANES):
        block = ms_ref[:, b * LANES:(b + 1) * LANES]
        padded = jnp.concatenate([block, jnp.zeros((LANES - CASES * COMP, LANES), jnp.float32)], axis=0)
        tab[b * LANES:(b + 1) * LANES, :] = padded.T
    sub = lax.broadcasted_iota(jnp.int32, (8, LANES), 0)

    @pl.loop(0, count // 32)
    def _(b):
        for g in range(4):
            entries = [nodes_ref[b * 32 + g * 8 + m] for m in range(8)]
            out_ref[b, g * 8:(g + 1) * 8, :] = merge_rows(tab, entries, sub)


def picked_rows(mode_shapes, send_nodes):
    count = send_nodes.shape[1]
    nodes = mode_shapes.shape[1]
    return pl.pallas_call(
        functools.partial(pick_kernel, count=count),
        in_specs=[pl.BlockSpec(memory_space=pltpu.SMEM), pl.BlockSpec(memory_space=pltpu.VMEM)],
        out_specs=pl.BlockSpec(memory_space=pltpu.VMEM),
        out_shape=jax.ShapeDtypeStruct((count // SLOT, SLOT, LANES), jnp.float32),
        scratch_shapes=[pltpu.VMEM((nodes, LANES), jnp.float32)],
        cost_estimate=pl.CostEstimate(flops=1_000_000, bytes_accessed=3_000_000, transcendentals=0),
        name="picked_rows",
    )(send_nodes.reshape(count), mode_shapes)


def flux_kernel(freq_ref, st_ref, up_ref, dn_ref, lf_ref, rt_ref, vol_ref, jac_ref, out_ref, q):
    step = pl.program_id(0)
    lane8 = lax.broadcasted_iota(jnp.int32, (8, LANES), 1)
    row8 = lax.broadcasted_iota(jnp.int32, (8, LANES), 0)
    dims = (((0,), (0,)), ((), ()))

    def outer(ref, at):
        values = jnp.broadcast_to(ref[...], (8, R2 * BI))
        spot = jnp.where((row8 == 0) & (lane8 == at), 1.0, 0.0)
        return lax.dot_general(values.astype(jnp.bfloat16), spot.astype(jnp.bfloat16), dims, preferred_element_type=jnp.float32)

    left = outer(lf_ref, LANES - 1)
    right = outer(rt_ref, 0)
    for r in range(R2):
        q[r * RPITCH + 8:r * RPITCH + 8 + BI, :] = left[r * BI:(r + 1) * BI]
        base = r * RPITCH + (TILES + 1) * PITCH + 8
        q[base:base + BI, :] = right[r * BI:(r + 1) * BI]
        for t in range(TILES):
            base = r * RPITCH + (t + 1) * PITCH + 8
            q[base:base + BI, :] = st_ref[r, :, t * LANES:(t + 1) * LANES].astype(jnp.float32)
    for t in range(TILES):
        lanes = slice(t * LANES, (t + 1) * LANES)
        base = (t + 1) * PITCH
        q[pl.ds(base + 7, R2, stride=RPITCH), :] = up_ref[:, lanes].astype(jnp.float32)
        q[pl.ds(base + 8 + BI, R2, stride=RPITCH), :] = dn_ref[:, lanes].astype(jnp.float32)

    first_lane = lane8 == 0
    last_lane = lane8 == LANES - 1

    @pl.loop(0, 2 * TILES * (CG // 2))
    def _(it):
        pair = it // (2 * TILES)
        pos = it % (2 * TILES)
        ti = pos // TILES
        tj = pos % TILES
        irows = pl.ds(pl.multiple_of(ti * 8, 8), 8)
        jlanes = pl.ds(pl.multiple_of(tj * LANES, LANES), LANES)
        base = pair * (2 * CASE_ROWS * RPITCH) + (tj + 1) * PITCH + 8 + ti * 8
        sets = [(cs, part) for cs in range(2) for part in range(2)]
        acc = [[None] * VARS for _ in sets]
        centers = {}

        def load(index, u, shift):
            r = index * VARS + u
            return q[pl.ds(base + r * RPITCH + shift, 8), :]

        for u in range(VARS):
            for b in range(5):
                values = []
                for index in range(4):
                    if b == 0:
                        x = load(index, u, 0)
                    elif b == 1:
                        x = load(index, u, -1)
                    elif b == 2:
                        x = load(index, u, 1)
                    elif b == 3:
                        here = pltpu.roll(load(index, u, 0), 1, 1)
                        x = jnp.where(first_lane, pltpu.roll(load(index, u, -PITCH), 1, 1), here)
                    else:
                        here = pltpu.roll(load(index, u, 0), LANES - 1, 1)
                        x = jnp.where(last_lane, pltpu.roll(load(index, u, PITCH), LANES - 1, 1), here)
                    values.append(x)
                for v in range(VARS):
                    block = jac_ref[b * VARS * VARS + v * VARS + u, irows, jlanes]
                    for index in range(4):
                        term = block * values[index]
                        old = acc[index][v]
                        acc[index][v] = term if old is None else old + term
        volume = vol_ref[irows, jlanes]
        for cs in range(2):
            scale = volume * freq_ref[step * CG + pair * 2 + cs]
            for v in range(VARS):
                real = load(cs * 2, v, 0)
                imag = load(cs * 2 + 1, v, 0)
                row = (pair * 2 + cs) * CASE_ROWS + v
                out_ref[row, irows, jlanes] = acc[cs * 2][v] - scale * imag
                out_ref[row + VARS, irows, jlanes] = acc[cs * 2 + 1][v] + scale * real


def flux_part(frequency, state, up, down, left, right, volume, jacobian):
    steps = CASES // CG
    whole = lambda i: (0, 0)
    return pl.pallas_call(
        flux_kernel,
        grid=(steps,),
        in_specs=[
            pl.BlockSpec(memory_space=pltpu.SMEM),
            pl.BlockSpec((R2, BI, BJ), lambda i: (i, 0, 0)),
            pl.BlockSpec((R2, BJ), lambda i: (i, 0)),
            pl.BlockSpec((R2, BJ), lambda i: (i, 0)),
            pl.BlockSpec((1, R2 * BI), lambda i: (0, i)),
            pl.BlockSpec((1, R2 * BI), lambda i: (0, i)),
            pl.BlockSpec((BI, BJ), whole),
            pl.BlockSpec((5 * VARS * VARS, BI, BJ), lambda i: (0, 0, 0)),
        ],
        out_specs=pl.BlockSpec((R2, BI, BJ), lambda i: (i, 0, 0)),
        out_shape=jax.ShapeDtypeStruct((ROWS, BI, BJ), jnp.float32),
        scratch_shapes=[pltpu.VMEM((R2 * RPITCH, LANES), jnp.float32)],
        cost_estimate=pl.CostEstimate(flops=140_000_000, bytes_accessed=20_000_000, transcendentals=0),
        name="flux_part",
    )(frequency, state, up, down, left, right, volume, jacobian)


def spread_kernel(freq_ref, entry_ref, index_ref, weight_ref, blend_ref, gain_ref, table_ref, flux_ref, motion_ref, out_ref, wsc, wt, acc, disp):
    total = jnp.zeros((8, LANES), jnp.float32)
    for k in range(KST):
        total = total + jnp.where(index_ref[k] >= 0, weight_ref[k], 0.0)
    ratio = blend_ref[...] / total
    for k in range(KST):
        wsc[k * 8:(k + 1) * 8, :] = jnp.where(index_ref[k] >= 0, weight_ref[k], 0.0) * ratio
    sub = lax.broadcasted_iota(jnp.int32, (8, LANES), 0)

    @pl.loop(0, 8)
    def _(s):
        mine = wsc[pl.ds(s, KST, stride=8), :]
        wide = jnp.concatenate([mine, jnp.zeros((LANES - KST, LANES), jnp.float32)], axis=0)
        wt[...] = wide.T

        @pl.loop(0, LANES // (8 * 1 * 16))
        def _(jo):
            seen = []
            for ji in range(16):
                jb = (jo * 16 + ji) * 1
                rows = [pl.ds(pl.multiple_of((jb + w) * 8, 8), 8) for w in range(1)]
                wide8 = [wt[r, :] for r in rows]
                sums = [None] * 1
                for k in range(KST):
                    base = s * (KST * LANES) + jb * 8 + k * LANES
                    if len(seen) >= 1:
                        base = base + (seen[-1] >> 31)
                    names = entry_ref.at[pl.ds(base, 8 * 1)]
                    entries = [names[m] for m in range(8 * 1)]
                    seen.append(entries[2])
                    for w in range(1):
                        value = merge_rows(table_ref, entries[w * 8:w * 8 + 8], sub) * jnp.broadcast_to(wide8[w][:, k:k + 1], (8, LANES))
                        sums[w] = value if sums[w] is None else sums[w] + value
                for w in range(1):
                    acc[rows[w], :] = sums[w]

        turned = acc[...].T
        for g in range(CASES * COMP // 8):
            disp[pl.ds(g * 64 + s, 8, stride=8), :] = turned[g * 8:(g + 1) * 8]

    gains = [gain_ref[i] for i in range(2 * VARS * COMP)]

    @pl.loop(0, CASES)
    def _(c):
        freq = freq_ref[c]
        parts = [disp[pl.ds(pl.multiple_of((c * COMP + x) * 8, 8), 8), :] for x in range(COMP)]
        for x in range(COMP):
            motion_ref[c * COMP + x] = parts[x]
        for v in range(VARS):
            pos = gains[v * COMP] * parts[0]
            vel = gains[(VARS + v) * COMP] * parts[0]
            for x in range(1, COMP):
                pos = pos + gains[v * COMP + x] * parts[x]
                vel = vel + gains[(VARS + v) * COMP + x] * parts[x]
            row = c * CASE_ROWS + v
            out_ref[row] = flux_ref[row] + pos
            out_ref[row + VARS] = flux_ref[row + VARS] + freq * vel


def spread_cells(frequency, entries, index, weight, blend, gain, table, flux):
    place = lambda i: (0, i // TILES, i % TILES)
    flat = lambda i: (i // TILES, i % TILES)
    return pl.pallas_call(
        spread_kernel,
        grid=(2 * TILES,),
        in_specs=[
            pl.BlockSpec(memory_space=pltpu.SMEM),
            pl.BlockSpec((KST * 8 * LANES,), lambda i: (i,), memory_space=pltpu.SMEM),
            pl.BlockSpec((KST, 8, LANES), place),
            pl.BlockSpec((KST, 8, LANES), place),
            pl.BlockSpec((8, LANES), flat),
            pl.BlockSpec((2 * VARS * COMP, 8, LANES), place),
            pl.BlockSpec(table.shape, lambda i: (0, 0)),
            pl.BlockSpec((ROWS, 8, LANES), place),
        ],
        out_specs=[
            pl.BlockSpec((CASES * COMP, 8, LANES), place),
            pl.BlockSpec((ROWS, 8, LANES), place),
        ],
        out_shape=[
            jax.ShapeDtypeStruct((CASES * COMP, BI, BJ), jnp.float32),
            jax.ShapeDtypeStruct((ROWS, BI, BJ), jnp.float32),
        ],
        scratch_shapes=[
            pltpu.VMEM((KST * 8, LANES), jnp.float32),
            pltpu.VMEM((LANES, LANES), jnp.float32),
            pltpu.VMEM((LANES, LANES), jnp.float32),
            pltpu.VMEM((CASES * COMP * 8, LANES), jnp.float32),
        ],
        cost_estimate=pl.CostEstimate(flops=40_000_000, bytes_accessed=28_000_000, transcendentals=0),
        compiler_params=pltpu.CompilerParams(),
        name="spread_cells",
    )(frequency, entries, index, weight, blend, gain, table, flux)


def shifted(value, axis, up):
    peers = lax.axis_size(axis)
    pairs = [(i, i + 1) for i in range(peers - 1)]
    return lax.ppermute(value, axis, pairs if up else [(j, i) for i, j in pairs])


def local(mode_shapes, send_nodes, interp_index, interp_weight, blend, motion_gain, frequency, volume, jacobian, state):
    first, last, left_col, right_col = halo_strips(state)
    mode_shapes, first, last, left_col, right_col = lax.optimization_barrier((mode_shapes, first, last, left_col, right_col))
    up = shifted(last, "group", True)
    down = shifted(first, "group", False)
    left = shifted(right_col, "dom", True)
    right = shifted(left_col, "dom", False)
    outgoing = picked_rows(mode_shapes, send_nodes)
    arrived = lax.all_to_all(outgoing, ("group", "dom"), split_axis=0, concat_axis=0, tiled=True)
    table = arrived.reshape(-1, LANES)
    safe = jnp.maximum(interp_index, 0)
    entries = safe.reshape(KST, 2, 8, TILES, LANES).transpose(1, 3, 2, 0, 4).reshape(-1)
    flux = flux_part(frequency, state, up, down, left, right, volume, jacobian)
    return tuple(spread_cells(frequency, entries, interp_index, interp_weight, blend, motion_gain, table, flux))


def solution(mesh):
    placed = (
        P(None, ("group", "dom")),
        P(("group", "dom"), None),
        P(None, "group", "dom"),
        P(None, "group", "dom"),
        P("group", "dom"),
        P(None, "group", "dom"),
        P(),
        P("group", "dom"),
        P(None, "group", "dom"),
        P(None, "group", "dom"),
    )
    return jax.shard_map(
        local,
        mesh=mesh,
        in_specs=placed,
        out_specs=(P(None, "group", "dom"), P(None, "group", "dom")),
        check_vma=False,
    )
```

```python
import functools

import jax
import jax.numpy as jnp
from jax import lax
from jax.experimental import pallas as pl
from jax.experimental.pallas import tpu as pltpu
from jax.sharding import PartitionSpec as P

COMP = 3
VARS = 5
CASES = 32
KST = 8
SLOT = 32
PACKED = 24
MEET = 3
HOP = 37
BI = 16
BJ = 512
LANES = 128
ROWS = CASES * 2 * VARS
TILES = BJ // LANES
CASE_ROWS = 2 * VARS
CG = 4
R2 = CG * CASE_ROWS
PITCH = 32
RPITCH = (TILES + 2) * PITCH


def merge_rows(table_ref, entries, sub):
    total = None
    for m, entry in enumerate(entries):
        row = table_ref[pl.ds(entry, 8, stride=0), :]
        total = row if total is None else jnp.where(sub == m, row, total)
    return total


def pick(nodes_ref, ms_ref, out_ref, tab, picked):
    nodes = ms_ref.shape[1]
    count = nodes_ref.shape[0]
    for b in range(nodes // LANES):
        block = ms_ref[:, b * LANES:(b + 1) * LANES]
        padded = jnp.concatenate([block, jnp.zeros((LANES - CASES * COMP, LANES), jnp.float32)], axis=0)
        tab[b * LANES:(b + 1) * LANES, :] = padded.T
    sub = lax.broadcasted_iota(jnp.int32, (8, LANES), 0)
    lane = lax.broadcasted_iota(jnp.int32, (8, LANES), 1)
    chunk = min(count, 512)

    @pl.loop(0, count // chunk)
    def _(b):
        seen = None
        for g in range(chunk // 8):
            base = b * chunk + g * 8
            if seen is not None:
                base = base + (seen >> 31)
            names = nodes_ref.at[pl.ds(base, 8)]
            entries = [names[m] for m in range(8)]
            seen = entries[2]
            picked[pl.ds(pl.multiple_of(b * chunk + g * 8, 8), 8), :] = merge_rows(tab, entries, sub)

    @pl.loop(0, count // SLOT, unroll=4)
    def _(b):
        groups = [picked[pl.ds(pl.multiple_of(b * SLOT + g * 8, 8), 8), :] for g in range(4)]
        for g in range(3):
            moved = pltpu.roll(groups[3], 96 - 32 * g, 1)
            out_ref[b, g * 8:(g + 1) * 8, :] = jnp.where(lane < 96, groups[g], moved)


def strips(st_ref, block, scr, first, last, lcol, rcol):
    n = R2 * BI
    for t in range(TILES):
        tile = st_ref[:, :, t * LANES:(t + 1) * LANES].astype(jnp.float32)
        scr[t] = tile.reshape(n, LANES)
    for t in range(TILES):
        lanes = slice(t * LANES, (t + 1) * LANES)
        first[block, :, lanes] = scr.at[t][pl.ds(0, R2, stride=BI), :].astype(jnp.bfloat16)
        last[block, :, lanes] = scr.at[t][pl.ds(BI - 1, R2, stride=BI), :].astype(jnp.bfloat16)
    lane = lax.broadcasted_iota(jnp.int32, (16, LANES), 1)
    dims = (((1,), (1,)), ((), ()))
    spot = jnp.where(lane == 0, 1.0, 0.0).astype(jnp.bfloat16)
    edge = st_ref[:, :, 0:LANES].reshape(n, LANES)
    lcol[block] = lax.dot_general(spot, edge, dims, preferred_element_type=jnp.float32)[0:1]
    spot = jnp.where(lane == LANES - 1, 1.0, 0.0).astype(jnp.bfloat16)
    edge = st_ref[:, :, BJ - LANES:BJ].reshape(n, LANES)
    rcol[block] = lax.dot_general(spot, edge, dims, preferred_element_type=jnp.float32)[0:1]


def flux_kernel(nodes_ref, freq_ref, st_ref, ms_any, vol_ref, jac_any, index_ref, out_ref, got_ref, names_ref,
                scr, first, last, lcol, rcol, up_ref, dn_ref, lf_ref, rt_ref, tab, picked, go_ref, ms_ref, jac_ref, q,
                strip_send, strip_recv, send, recv, own, load):
    grid_step = pl.program_id(0)
    blocks = CASES // CG
    step = lax.rem(grid_step, blocks)
    groups, doms = lax.axis_size("group"), lax.axis_size("dom")
    g, d = lax.axis_index("group"), lax.axis_index("dom")
    peers = groups * doms
    me = g * doms + d
    mesh_ids = pl.DeviceIdType.MESH

    def peer_of(i):
        other = lax.rem(me + i, peers)
        return other, {"group": other // doms, "dom": lax.rem(other, doms)}

    above, below = {"group": lax.rem(g + 1, groups)}, {"group": lax.rem(g + groups - 1, groups)}
    after, before = {"dom": lax.rem(d + 1, doms)}, {"dom": lax.rem(d + doms - 1, doms)}
    moves = [(last, up_ref, above), (first, dn_ref, below), (rcol, lf_ref, after), (lcol, rt_ref, before)]

    def strip_copies(block):
        return [
            pltpu.make_async_remote_copy(
                src_ref=src.at[block], dst_ref=dst.at[block], send_sem=strip_send.at[i, block], recv_sem=strip_recv.at[i, block],
                device_id=peer, device_id_type=mesh_ids)
            for i, (src, dst, peer) in enumerate(moves)
        ]

    def send_strips(block):
        for copy in strip_copies(block):
            copy.start()

    mine = pltpu.make_async_copy(go_ref.at[me], got_ref.at[me], own)
    shapes_in = pltpu.make_async_copy(ms_any, ms_ref, load.at[0])
    blocks_in = pltpu.make_async_copy(jac_any, jac_ref, load.at[1])

    @pl.when(grid_step == 0)
    def _():
        barrier = pltpu.get_barrier_semaphore()

        @pl.loop(1, peers)
        def _(i):
            pl.semaphore_signal(barrier, inc=1, device_id=peer_of(i)[1], device_id_type=mesh_ids)

        shapes_in.start()

    @pl.when(grid_step == MEET)
    def _():
        pl.semaphore_wait(pltpu.get_barrier_semaphore(), peers - 1)
        for block in range(MEET):
            send_strips(block)

    @pl.when((grid_step > MEET) & (grid_step <= blocks))
    def _():
        send_strips(grid_step - 1)

    @pl.when(grid_step < blocks)
    def _():
        strips(st_ref, step, scr, first, last, lcol, rcol)

    @pl.when(grid_step == blocks - 1)
    def _():
        blocks_in.start()
        shapes_in.wait()
        pick(nodes_ref, ms_ref, go_ref, tab, picked)
        for p in range(2 * TILES):
            ti, tj = p // TILES, p % TILES
            for k in range(KST):
                entry = index_ref[k, ti * 8:ti * 8 + 8, tj * LANES:(tj + 1) * LANES]
                names_ref[pl.ds(p * 64 + k, 8, stride=8), :] = jnp.maximum(entry, 0)

    @pl.when(grid_step == blocks)
    def _():
        @pl.loop(1, peers)
        def _(i):
            other, where = peer_of(lax.rem(i * HOP, peers))
            pltpu.make_async_remote_copy(
                src_ref=go_ref.at[other], dst_ref=got_ref.at[me], send_sem=send, recv_sem=recv,
                device_id=where, device_id_type=mesh_ids).start()

        mine.start()
        blocks_in.wait()

    @pl.when(grid_step >= blocks)
    def _():
        for copy in strip_copies(step):
            copy.wait()
        flux_block(freq_ref, st_ref, up_ref, dn_ref, lf_ref, rt_ref, vol_ref, jac_ref, out_ref, q, step, g, d, groups, doms)

    @pl.when(grid_step == 2 * blocks - 1)
    def _():
        some = pl.ds(0, peers - 1)
        mine.wait()
        pltpu.make_async_copy(go_ref.at[some], got_ref.at[some], send).wait()
        pltpu.make_async_copy(go_ref.at[some], got_ref.at[some], recv).wait()


def flux_block(freq_ref, st_ref, up_ref, dn_ref, lf_ref, rt_ref, vol_ref, jac_ref, out_ref, q, step, g, d, groups, doms):
    lane8 = lax.broadcasted_iota(jnp.int32, (8, LANES), 1)
    row8 = lax.broadcasted_iota(jnp.int32, (8, LANES), 0)
    dims = (((0,), (0,)), ((), ()))

    def outer(ref, at):
        values = jnp.broadcast_to(ref[step], (8, R2 * BI))
        spot = jnp.where((row8 == 0) & (lane8 == at), 1.0, 0.0)
        return lax.dot_general(values.astype(jnp.bfloat16), spot.astype(jnp.bfloat16), dims, preferred_element_type=jnp.float32)

    left = outer(lf_ref, LANES - 1) * jnp.where(d > 0, 1.0, 0.0)
    right = outer(rt_ref, 0) * jnp.where(d < doms - 1, 1.0, 0.0)
    has_up = jnp.where(g > 0, 1.0, 0.0)
    has_dn = jnp.where(g < groups - 1, 1.0, 0.0)
    for r in range(R2):
        q[r * RPITCH + 8:r * RPITCH + 8 + BI, :] = left[r * BI:(r + 1) * BI]
        base = r * RPITCH + (TILES + 1) * PITCH + 8
        q[base:base + BI, :] = right[r * BI:(r + 1) * BI]
        for t in range(TILES):
            base = r * RPITCH + (t + 1) * PITCH + 8
            q[base:base + BI, :] = st_ref[r, :, t * LANES:(t + 1) * LANES].astype(jnp.float32)
    for t in range(TILES):
        lanes = slice(t * LANES, (t + 1) * LANES)
        base = (t + 1) * PITCH
        q[pl.ds(base + 7, R2, stride=RPITCH), :] = up_ref[step, :, lanes].astype(jnp.float32) * has_up
        q[pl.ds(base + 8 + BI, R2, stride=RPITCH), :] = dn_ref[step, :, lanes].astype(jnp.float32) * has_dn

    first_lane = lane8 == 0
    last_lane = lane8 == LANES - 1

    def flux_case(pair, ti, tj):
        irows = pl.ds(pl.multiple_of(ti * 8, 8), 8)
        jlanes = pl.ds(pl.multiple_of(tj * LANES, LANES), LANES)
        base = pair * (CASE_ROWS * RPITCH) + (tj + 1) * PITCH + 8 + ti * 8
        sets = [(cs, part) for cs in range(1) for part in range(2)]
        acc = [[None] * VARS for _ in sets]
        centers = {}

        def load(index, u, shift):
            r = index * VARS + u
            return q[pl.ds(base + r * RPITCH + shift, 8), :]

        for b in (0, 1, 2, 3, 4):
            for u in range(VARS):
                values = []
                for index in range(2):
                    if b == 0:
                        x = load(index, u, 0)
                    elif b == 1:
                        x = load(index, u, -1)
                    elif b == 2:
                        x = load(index, u, 1)
                    elif b == 3:
                        x = pltpu.roll(jnp.where(last_lane, load(index, u, -PITCH), load(index, u, 0)), 1, 1)
                    else:
                        x = pltpu.roll(jnp.where(first_lane, load(index, u, PITCH), load(index, u, 0)), LANES - 1, 1)
                    values.append(x)
                for v in range(VARS):
                    block = jac_ref[b * VARS * VARS + v * VARS + u, irows, jlanes]
                    for index in range(2):
                        term = block * values[index]
                        old = acc[index][v]
                        acc[index][v] = term if old is None else old + term
        volume = vol_ref[irows, jlanes]
        for cs in range(1):
            scale = volume * freq_ref[step * CG + pair + cs]
            for v in range(VARS):
                real = load(cs * 2, v, 0)
                imag = load(cs * 2 + 1, v, 0)
                row = (pair + cs) * CASE_ROWS + v
                out_ref[row, irows, jlanes] = acc[cs * 2][v] - scale * imag
                out_ref[row + VARS, irows, jlanes] = acc[cs * 2 + 1][v] + scale * real

    @pl.loop(0, 2 * TILES * CG // 2)
    def _(it):
        for sub in range(2):
            pos = it % (2 * TILES)
            flux_case(it // (2 * TILES) * 2 + sub, pos // TILES, pos % TILES)


def flux_part(send_nodes, frequency, state, mode_shapes, volume, jacobian, index):
    blocks = CASES // CG
    count = send_nodes.shape[1]
    nodes = mode_shapes.shape[1]
    anywhere = pl.BlockSpec(memory_space=pl.ANY)
    scalars = pl.BlockSpec(memory_space=pltpu.SMEM)
    rows = (count // SLOT, PACKED, LANES)
    cols = (blocks, 1, R2 * BI)
    return pl.pallas_call(
        flux_kernel,
        grid=(2 * blocks,),
        in_specs=[
            scalars,
            scalars,
            pl.BlockSpec((R2, BI, BJ), lambda i: (lax.rem(i, blocks), 0, 0)),
            anywhere,
            pl.BlockSpec((BI, BJ), lambda i: (0, 0)),
            anywhere,
            pl.BlockSpec((KST, BI, BJ), lambda i: (0, 0, 0)),
        ],
        out_specs=[
            pl.BlockSpec((R2, BI, BJ), lambda i: (jnp.maximum(i - blocks, 0), 0, 0)),
            anywhere,
            pl.BlockSpec((KST * BI * TILES, LANES), lambda i: (0, 0)),
        ],
        out_shape=[
            jax.ShapeDtypeStruct((ROWS, BI, BJ), jnp.float32),
            jax.ShapeDtypeStruct(rows, jnp.float32),
            jax.ShapeDtypeStruct((KST * BI * TILES, LANES), jnp.int32),
        ],
        scratch_shapes=[
            pltpu.VMEM((TILES, R2 * BI, LANES), jnp.float32),
            pltpu.VMEM((blocks, R2, BJ), jnp.bfloat16),
            pltpu.VMEM((blocks, R2, BJ), jnp.bfloat16),
            pltpu.VMEM(cols, jnp.float32),
            pltpu.VMEM(cols, jnp.float32),
            pltpu.VMEM((blocks, R2, BJ), jnp.bfloat16),
            pltpu.VMEM((blocks, R2, BJ), jnp.bfloat16),
            pltpu.VMEM(cols, jnp.float32),
            pltpu.VMEM(cols, jnp.float32),
            pltpu.VMEM((nodes, LANES), jnp.float32),
            pltpu.VMEM((count, LANES), jnp.float32),
            pltpu.VMEM(rows, jnp.float32),
            pltpu.VMEM(mode_shapes.shape, jnp.float32),
            pltpu.VMEM(jacobian.shape, jnp.float32),
            pltpu.VMEM((R2 * RPITCH, LANES), jnp.float32),
            pltpu.SemaphoreType.DMA((4, blocks)),
            pltpu.SemaphoreType.DMA((4, blocks)),
            pltpu.SemaphoreType.DMA,
            pltpu.SemaphoreType.DMA,
            pltpu.SemaphoreType.DMA,
            pltpu.SemaphoreType.DMA((2,)),
        ],
        compiler_params=pltpu.CompilerParams(collective_id=0, has_side_effects=True),
        cost_estimate=pl.CostEstimate(flops=140_000_000, bytes_accessed=28_000_000, transcendentals=0),
        name="flux_part",
    )(send_nodes.reshape(count), frequency, state, mode_shapes, volume, jacobian, index)


def unpack(packed_ref, table_ref):
    lane = lax.broadcasted_iota(jnp.int32, (8, LANES), 1)

    @pl.when(pl.program_id(0) == 0)
    def _():
        @pl.loop(0, packed_ref.shape[0], unroll=4)
        def _(b):
            groups = [packed_ref[b, g * 8:(g + 1) * 8, :] for g in range(3)]
            for g in range(3):
                table_ref[pl.ds(pl.multiple_of(b * SLOT + g * 8, 8), 8), :] = groups[g]
            moved = [pltpu.roll(groups[g], 32 + 32 * g, 1) for g in range(3)]
            last = jnp.where(lane < 32, moved[0], jnp.where(lane < 64, moved[1], moved[2]))
            table_ref[pl.ds(pl.multiple_of(b * SLOT + 24, 8), 8), :] = last


def spread_kernel(freq_ref, entry_ref, index_ref, weight_ref, blend_ref, gain_ref, packed_ref, flux_ref, motion_ref, out_ref, wsc, wt, acc, disp, table_ref):
    place = pl.program_id(0)
    places = pl.num_programs(0) - 1
    now = lax.rem(place, 2)
    half = CASES * COMP * 8
    unpack(packed_ref, table_ref)
    total = jnp.zeros((8, LANES), jnp.float32)
    for k in range(KST):
        total = total + jnp.where(index_ref[k] >= 0, weight_ref[k], 0.0)
    ratio = blend_ref[...] / total
    for k in range(KST):
        wsc[k * 8:(k + 1) * 8, :] = jnp.where(index_ref[k] >= 0, weight_ref[k], 0.0) * ratio
    sub = lax.broadcasted_iota(jnp.int32, (8, LANES), 0)

    def turn_weights(s, slot):
        mine = wsc[pl.ds(s, KST, stride=8), :]
        wide = jnp.concatenate([mine, jnp.zeros((LANES - KST, LANES), jnp.float32)], axis=0)
        wt[pl.ds(pl.multiple_of(slot * LANES, 8), LANES), :] = wide.T

    def turn_sums(s, slot):
        turned = acc[pl.ds(pl.multiple_of(slot * LANES, 8), LANES), :].T
        for g in range(CASES * COMP // 8):
            disp[pl.ds(now * half + g * 64 + s, 8, stride=8), :] = turned[g * 8:(g + 1) * 8]

    def residual(c):
        freq = freq_ref[c]
        start = (1 - now) * half
        parts = [disp[pl.ds(pl.multiple_of(start + (c * COMP + x) * 8, 8), 8), :] for x in range(COMP)]
        for x in range(COMP):
            motion_ref[c * COMP + x] = parts[x]
        for v in range(VARS):
            pos = gain_ref[v * COMP] * parts[0]
            vel = gain_ref[(VARS + v) * COMP] * parts[0]
            for x in range(1, COMP):
                pos = pos + gain_ref[v * COMP + x] * parts[x]
                vel = vel + gain_ref[(VARS + v) * COMP + x] * parts[x]
            row = c * CASE_ROWS + v
            out_ref[row] = flux_ref[row] + pos
            out_ref[row + VARS] = flux_ref[row + VARS] + freq * vel

    @pl.when(place < places)
    def _():
        turn_weights(0, 0)

        @pl.loop(0, 8)
        def _(s):
            slot = lax.rem(s, 2)
            for c in range(CASES // 8):
                residual(s * (CASES // 8) + c)
            turn_sums(lax.rem(s + 7, 8), 1 - slot)
            seen = None
            block = entry_ref.at[pl.ds(s * (KST * LANES), KST * LANES)]
            for jb in range(LANES // 8):
                rows = pl.ds(pl.multiple_of(slot * LANES + jb * 8, 8), 8)
                wide8 = wt[rows, :]
                sums = None
                for k in range(KST):
                    base = jb * 8 + k * LANES
                    if seen is not None:
                        base = base + delay
                    names = block.at[pl.ds(base, 8)]
                    entries = [names[m] for m in range(8)]
                    if seen is None or k % 1 == 1 - 1:
                        seen = entries[0]
                        delay = seen >> 31
                    value = merge_rows(table_ref, entries, sub) * jnp.broadcast_to(wide8[:, k:k + 1], (8, LANES))
                    sums = value if sums is None else sums + value
                acc[rows, :] = sums
            turn_weights(jnp.minimum(s + 1, 7), 1 - slot)

        turn_sums(7, 1)

    @pl.when(place == places)
    def _():
        @pl.loop(0, CASES)
        def _(c):
            residual(c)


def spread_cells(frequency, entries, index, weight, blend, gain, table, flux):
    places = 2 * TILES

    def coming(i):
        return jnp.minimum(i, places - 1)

    def going(i):
        return jnp.maximum(i - 1, 0)

    def split(i):
        return (i // TILES, i % TILES)

    return pl.pallas_call(
        spread_kernel,
        grid=(places + 1,),
        in_specs=[
            pl.BlockSpec(memory_space=pltpu.SMEM),
            pl.BlockSpec((KST * 8 * LANES,), lambda i: (coming(i),), memory_space=pltpu.SMEM),
            pl.BlockSpec((KST, 8, LANES), lambda i: (0, *split(coming(i)))),
            pl.BlockSpec((KST, 8, LANES), lambda i: (0, *split(coming(i)))),
            pl.BlockSpec((8, LANES), lambda i: split(coming(i))),
            pl.BlockSpec((2 * VARS * COMP, 8, LANES), lambda i: (0, *split(going(i)))),
            pl.BlockSpec(table.shape, lambda i: (0, 0, 0)),
            pl.BlockSpec((ROWS, 8, LANES), lambda i: (0, *split(going(i)))),
        ],
        out_specs=[
            pl.BlockSpec((CASES * COMP, 8, LANES), lambda i: (0, *split(going(i)))),
            pl.BlockSpec((ROWS, 8, LANES), lambda i: (0, *split(going(i)))),
        ],
        out_shape=[
            jax.ShapeDtypeStruct((CASES * COMP, BI, BJ), jnp.float32),
            jax.ShapeDtypeStruct((ROWS, BI, BJ), jnp.float32),
        ],
        scratch_shapes=[
            pltpu.VMEM((KST * 8, LANES), jnp.float32),
            pltpu.VMEM((2 * LANES, LANES), jnp.float32),
            pltpu.VMEM((2 * LANES, LANES), jnp.float32),
            pltpu.VMEM((2 * CASES * COMP * 8, LANES), jnp.float32),
            pltpu.VMEM((table.shape[0] * SLOT, LANES), jnp.float32),
        ],
        cost_estimate=pl.CostEstimate(flops=40_000_000, bytes_accessed=28_000_000, transcendentals=0),
        compiler_params=pltpu.CompilerParams(),
        name="spread_cells",
    )(frequency, entries, index, weight, blend, gain, table, flux)


def local(mode_shapes, send_nodes, interp_index, interp_weight, blend, motion_gain, frequency, volume, jacobian, state):
    flux, arrived, names = flux_part(send_nodes, frequency, state, mode_shapes, volume, jacobian, interp_index)
    entries = names.reshape(-1)
    return tuple(spread_cells(frequency, entries, interp_index, interp_weight, blend, motion_gain, arrived, flux))


def solution(mesh):
    placed = (
        P(None, ("group", "dom")),
        P(("group", "dom"), None),
        P(None, "group", "dom"),
        P(None, "group", "dom"),
        P("group", "dom"),
        P(None, "group", "dom"),
        P(),
        P("group", "dom"),
        P(None, "group", "dom"),
        P(None, "group", "dom"),
    )
    return jax.shard_map(
        local,
        mesh=mesh,
        in_specs=placed,
        out_specs=(P(None, "group", "dom"), P(None, "group", "dom")),
        check_vma=False,
    )
```
